128 devices in a mesh: grp: 4 (over z_hi, core), blk: 32 (over x, z_lo, y).
Axes of the slice: x: 4, y: 4, z: 4 (z_hi: 2, z_lo: 2; z = z_hi * 2 + z_lo), core: 2. Of those that a mesh axis runs over, the one named last changes fastest.
Arguments:
- integrals: bfloat16 [32768, 32768], P('blk', 'grp'), may hold values from -0.046875 to 0.046875
- block_mask: int32 [256, 256], P('blk', 'grp'), may hold values from 0 to 1, as said below
- amplitudes: bfloat16 [32768, 1024], P(('grp', 'blk')), may hold values from -6 to 6
- pair_batches: int32 [8], replicated, may hold values from 0 to 7, each once
Outputs:
- ladder: bfloat16 [1024, 32768], P('grp', 'blk')
The draws below stay inside these ranges and needn't reach their ends.
Inputs may be any that keep to these rules, and one draw needn't show every extreme that they name: `block_mask`: 0 or 1; the share of kept tiles rises from about a quarter in the first tile row to about three quarters in the last. `pair_batches`: each batch number once.
All inputs are finite; a program needn't handle non-finite values.
Results may differ from the reference program's by a relative error of at most 0.001.
Values may be sent and summed in bfloat16 or wider, within the bound.
No kernel may reach another device: no remote copies, remote signals or barrier semaphores. Data moves between devices by JAX's collectives and lax.ppermute only.
A program may use at most 128 MiB of HBM per device.

```python
import jax
import jax.numpy as jnp
from jax import lax

BLOCK = 128
CD = 32768
BATCH = 128
NB = 8
AB_DEV = 1024
AB = 32768


def draw_block_mask(key, part):
    tile_rows = AB // BLOCK
    tile_cols = CD // BLOCK
    scores = jax.random.randint(jax.random.fold_in(key, 17), (tile_rows, tile_cols), 0, 1000)
    row_index = jnp.arange(tile_rows, dtype=jnp.int32)[:, None]
    limits = 250 + 500 * row_index // max(tile_rows - 1, 1)
    return (scores < limits).astype(jnp.int32)


def shard_levels(key, extent, shards, least, high):
    level, own = 1.0, jax.random.fold_in(key, 6)
    for axis_at, blocks in shards:
        steps = jnp.exp(jax.random.uniform(jax.random.fold_in(own, axis_at), (blocks,), jnp.float32, least / len(shards), high / len(shards)))
        level = level * jnp.repeat(steps, extent[axis_at] // blocks).reshape([-1 if axis == axis_at else 1 for axis in range(len(extent))])
    return level


def centred(own_key, dims, deviation, reach, split=(), held_as=jnp.bfloat16):
    drawn = jax.random.normal(own_key, dims, jnp.float32) * deviation
    if len(split) > 0:
        drawn = shard_levels(own_key, dims, split, -0.22, 0.18) * drawn
    return jnp.clip(drawn, min=-reach, max=reach).astype(held_as)


def setup_inputs(seed: int = 0) -> dict:
    streams_of = jax.random.split(jax.random.key(seed), 5)
    integrals = centred(streams_of[0], (AB, CD), (CD // 2) ** -0.5, 0.046875, ((0, 32), (1, 4)))
    block_mask = draw_block_mask(jax.random.fold_in(streams_of[4], 71), 0)
    amplitudes = centred(streams_of[2], (CD, NB * BATCH), 1.0, 6.0, ((0, 128),))
    pair_batches = jax.random.permutation(streams_of[3], NB).astype(jnp.int32)
    return dict(integrals=integrals, block_mask=block_mask, amplitudes=amplitudes, pair_batches=pair_batches)


def reference(integrals, block_mask, amplitudes, pair_batches):
    rows_in = amplitudes.shape[0]
    grouped = amplitudes.reshape(rows_in, NB, BATCH)
    chosen = jnp.take(grouped, pair_batches.astype(jnp.int32), axis=1).reshape(rows_in, NB * BATCH)
    rows_total = integrals.shape[0]
    widths = integrals.shape[1]
    steps_total = rows_total // AB_DEV

    def one_slab(position):
        vrows = lax.dynamic_slice_in_dim(integrals, position * AB_DEV, AB_DEV, 0)
        mrows = lax.dynamic_slice_in_dim(block_mask, position * (AB_DEV // BLOCK), AB_DEV // BLOCK, 0)
        weights = mrows.astype(integrals.dtype)[:, None, :, None]
        masked = (vrows.reshape(AB_DEV // BLOCK, BLOCK, widths // BLOCK, BLOCK) * weights).reshape(AB_DEV, widths)
        return lax.dot_general(chosen, masked, (((0,), (1,)), ((), ())), preferred_element_type=jnp.float32)

    slabs = lax.map(one_slab, jnp.arange(steps_total, dtype=jnp.int32))
    result = jnp.transpose(slabs, (1, 0, 2)).reshape(NB * BATCH, rows_total)
    return result.astype(jnp.bfloat16)
```

```python
import functools

import jax
import jax.numpy as jnp
from jax import lax
from jax.experimental import pallas as pl
from jax.experimental.pallas import tpu as pltpu
from jax.sharding import PartitionSpec as P

BLOCK = 128
BATCH = 128
NB = 8
NX, NZ, NY = 4, 2, 4
F32, BF16 = jnp.float32, jnp.bfloat16


def blk(x, z, y):
    return (x % NX) * (NZ * NY) + z * NY + y % NY


def perm(dx, dz, dy):
    cells = [(x, z, y) for x in range(NX) for z in range(NZ) for y in range(NY)]
    return [(blk(x, z, y), blk(x + dx, z ^ dz, y + dy)) for x, z, y in cells]


XP, XM, YP, YM, ZX = perm(1, 0, 0), perm(-1, 0, 0), perm(0, 0, 1), perm(0, 0, -1), perm(0, 1, 0)
CORE = [(g, g ^ 1) for g in range(4)]
ZHI = [(g, g ^ 2) for g in range(4)]
NT = (((1,), (1,)), ((), ()))


def send(array, pairs):
    return lax.ppermute(array, "blk", pairs)


def pick_kernel(order, amp_ref, out_ref):
    out_ref[...] = amp_ref[...].T


def pick(amplitudes, order):
    rows = amplitudes.shape[0]
    return pl.pallas_call(
        pick_kernel,
        out_shape=jax.ShapeDtypeStruct((NB * BATCH, rows), BF16),
        grid_spec=pltpu.PrefetchScalarGridSpec(
            num_scalar_prefetch=1,
            grid=(NB,),
            in_specs=[pl.BlockSpec((rows, BATCH), lambda k, order: (0, order[k]))],
            out_specs=pl.BlockSpec((BATCH, rows), lambda k, order: (k, 0)),
        ),
        cost_estimate=pl.CostEstimate(flops=1000000, bytes_accessed=1 << 20, transcendentals=0),
        name="pick",
    )(order, amplitudes)


def kept(v_ref, mask_ref, column, n):
    rows = []
    for r in range(2):
        cells = []
        for c in range(2):
            tile = v_ref[pl.ds(pl.multiple_of(n * 256 + r * 128, 128), 128), c * 128 : (c + 1) * 128]
            keep = mask_ref[n * 2 + r, column * 2 + c] != 0
            cells.append(jnp.where(keep, tile, jnp.zeros_like(tile)))
        rows.append(jnp.concatenate(cells, axis=1))
    return jnp.concatenate(rows, axis=0)


def cross_kernel(n_full, source, mask_ref, *refs):
    fulls, (x2a, x2b, y2a, y2b), v_ref, acc_ref = refs[:n_full], refs[n_full : n_full + 4], refs[-2], refs[-1]
    step = pl.program_id(0)
    column = source[step]

    @pl.when(step == 0)
    def _():
        acc_ref[...] = jnp.zeros_like(acc_ref)

    def update(parts):
        def body(n, carry):
            tile = kept(v_ref, mask_ref, column, n)
            at = pl.ds(pl.multiple_of(n * 256, 256), 256)
            row = 0
            for part in parts:
                size = part.shape[0]
                acc_ref[row : row + size, at] += lax.dot_general(
                    part[...], tile, NT, preferred_element_type=F32
                )
                row += size
            return carry

        lax.fori_loop(0, acc_ref.shape[1] // 256, body, 0)

    for i, full in enumerate(fulls):
        pl.when(step == i)(functools.partial(update, [full]))
    for i, (a, b) in enumerate([(x2a, x2b), (y2a, y2b)]):
        for k in range(2):
            pl.when(step == n_full + 2 * i + k)(functools.partial(update, [a.at[k], b.at[k]]))


def cross(fulls, seconds, v, mask, source):
    rows, depth = v.shape
    n_full = len(fulls)
    steps = n_full + 4
    whole = lambda a: pl.BlockSpec(a.shape, lambda i, s, m, nd=a.ndim: (0,) * nd, pipeline_mode=pl.Buffered(1))
    return pl.pallas_call(
        functools.partial(cross_kernel, n_full),
        out_shape=jax.ShapeDtypeStruct((NB * BATCH, rows), F32),
        grid_spec=pltpu.PrefetchScalarGridSpec(
            num_scalar_prefetch=2,
            grid=(steps,),
            in_specs=[whole(a) for a in fulls + seconds]
            + [pl.BlockSpec((rows, 256), lambda i, s, m: (0, s[i]))],
            out_specs=pl.BlockSpec((NB * BATCH, rows), lambda i, s, m: (0, 0), pipeline_mode=pl.Buffered(1)),
        ),
        cost_estimate=pl.CostEstimate(
            flops=2 * rows * steps * 256 * 1024, bytes_accessed=steps * (1 << 20), transcendentals=0
        ),
        name="cross",
    )(source, mask, *fulls, *seconds, v)


def group_kernel(source, mask_ref, ym, yp, y2, xm, xp, x2, v_ref, acc_a, acc_b, out_a, out_b):
    step = pl.program_id(0)
    column = source[step]
    dy, dx = step // 6, (step // 2) % 3

    @pl.when(step == 0)
    def _():
        out_a[...] = acc_a[...]
        out_b[...] = acc_b[...]

    def choose(which, refs):
        first, second, third = [r[0] for r in refs]
        return jnp.where(which == 0, first, jnp.where(which == 1, second, third))

    lhs = jnp.concatenate([choose(dy, (ym, yp, y2)), choose(dx, (xm, xp, x2))], axis=0)
    half = out_a.shape[0]

    def body(n, carry):
        tile = kept(v_ref, mask_ref, column, n)
        at = pl.ds(pl.multiple_of(n * 256, 256), 256)
        product = lax.dot_general(lhs, tile, NT, preferred_element_type=F32)
        out_a[:, at] += product[:half]
        out_b[:, at] += product[half:]
        return carry

    lax.fori_loop(0, out_a.shape[1] // 256, body, 0)


def group(index, ys, xs, v, mask, source, acc):
    rows, depth = v.shape
    cols = ys[0].shape[1]

    def y_map(which):
        def at(i, s, m):
            dy = i // 6
            return jnp.where(dy == which, i % 6, jnp.where(dy < which, 0, 5)), 0, 0

        return at

    def x_map(which):
        def at(i, s, m):
            dy, dx, dz = i // 6, (i // 2) % 3, i % 2
            return dy * 2 + jnp.where(dx == which, dz, jnp.where(dx < which, 0, 1)), 0, 0

        return at

    out = jax.ShapeDtypeStruct((cols, rows), F32)
    once = pl.Buffered(1)
    return pl.pallas_call(
        group_kernel,
        out_shape=(out, out),
        grid_spec=pltpu.PrefetchScalarGridSpec(
            num_scalar_prefetch=2,
            grid=(18,),
            in_specs=[pl.BlockSpec((1, cols, 256), y_map(k)) for k in range(3)]
            + [pl.BlockSpec((1, cols, 256), x_map(k)) for k in range(3)]
            + [pl.BlockSpec((rows, 256), lambda i, s, m: (0, s[i]))]
            + [
                pl.BlockSpec((cols, rows), lambda i, s, m, k=k: (k, 0), pipeline_mode=once)
                for k in (index, 2 + index)
            ],
            out_specs=[pl.BlockSpec((cols, rows), lambda i, s, m: (0, 0), pipeline_mode=once)] * 2,
        ),
        cost_estimate=pl.CostEstimate(
            flops=2 * rows * 18 * 256 * 512, bytes_accessed=18 * (1 << 20), transcendentals=0
        ),
        name="group%d" % index,
    )(source, mask, *ys, *xs, v, acc, acc)


def on_device(integrals, block_mask, amplitudes, pair_batches):
    b, g = lax.axis_index("blk"), lax.axis_index("grp")
    x, z, y = b // (NZ * NY), (b // NY) % NZ, b % NY

    place = jnp.arange(NB, dtype=jnp.int32)
    owner = g ^ (2 * (place & 1)) ^ (place >> 2)
    own = pick(amplitudes, pair_batches[2 * owner + ((place >> 1) & 1)])

    def sources(cells):
        dx, dz, dy = jnp.array(cells, jnp.int32).T
        return blk(x + dx, z ^ dz, y + dy)

    near = send(own, ZX)
    xm0, xp0, ym0, yp0 = send(own, XP), send(own, XM), send(own, YP), send(own, YM)
    xm1, xp1, ym1, yp1 = send(near, XP), send(near, XM), send(near, YP), send(near, YM)
    x2a = send(jnp.stack([xm0[:512], xm1[:512]]), XP)
    x2b = send(jnp.stack([xp0[512:], xp1[512:]]), XM)
    y2a = send(jnp.stack([ym0[:512], ym1[:512]]), YP)
    y2b = send(jnp.stack([yp0[512:], yp1[512:]]), YM)

    def line(arrays, second, at, at2):
        return jnp.stack([a[at : at + 256] for a in arrays] + [second[k, at2 : at2 + 256] for k in range(2)])

    pieces = []
    for k in range(2):
        along_x = line([xm0, xm1, xp0, xp1], x2a, 256 * k, 256 * k)
        along_y = line([ym0, ym1, yp0, yp1], y2b, 512 + 256 * k, 256 * k)
        ym, yp = send(along_x, YP), send(along_x, YM)
        xm, xp = send(along_y, XP), send(along_y, XM)
        y2, x2 = (send(ym, YP), send(xm, XP)) if k == 0 else (send(yp, YM), send(xp, XM))
        pieces.append(([ym, yp, y2], [xm, xp, x2]))

    full_at = [(0, 0, 0), (0, 1, 0)]
    full_at += [(dx, dz, 0) for dz in (0, 1) for dx in (-1, 1)]
    full_at += [(0, dz, dy) for dz in (0, 1) for dy in (-1, 1)]
    full_at += [(2, 0, 0), (2, 1, 0), (0, 0, 2), (0, 1, 2)]
    cross_source = sources(full_at)
    fulls = [own, near, xm0, xp0, xm1, xp1, ym0, yp0, ym1, yp1]
    acc = cross(fulls, [x2a, x2b, y2a, y2b], integrals, block_mask, cross_source)

    source = sources([(dx, dz, dy) for dy in (-1, 1, 2) for dx in (-1, 1, 2) for dz in (0, 1)])
    outs = []
    for k in range(2):
        mine, theirs = group(k, *pieces[k], integrals, block_mask, source, acc)
        got = lax.ppermute(theirs, "grp", CORE)
        far = lax.ppermute(mine[BATCH:] + got[BATCH:], "grp", ZHI)
        outs.append(mine[:BATCH] + got[:BATCH] + far)
    return jnp.concatenate(outs, axis=0).astype(BF16)


def solution(mesh):
    in_specs = (P("blk", "grp"), P("blk", "grp"), P(("grp", "blk"), None), P())
    out_specs = P("grp", "blk")
    return jax.shard_map(
        on_device, mesh=mesh, in_specs=in_specs, out_specs=out_specs, check_vma=False
    )
```

```python
import functools

import jax
import jax.numpy as jnp
from jax import lax
from jax.experimental import pallas as pl
from jax.experimental.pallas import tpu as pltpu
from jax.sharding import PartitionSpec as P


BLOCK = 128
BATCH = 128
NB = 8
NX, NZ, NY = 4, 2, 4
F32, BF16 = jnp.float32, jnp.bfloat16

LIMIT = 6 << 20
LINE = (-1, 1, 2)


def blk(x, z, y):
    return (x % NX) * (NZ * NY) + z * NY + y % NY


def perm(dx, dz, dy):
    cells = [(x, z, y) for x in range(NX) for z in range(NZ) for y in range(NY)]
    return [(blk(x, z, y), blk(x + dx, z ^ dz, y + dy)) for x, z, y in cells]


XP, XM, YP, YM, ZX = perm(1, 0, 0), perm(-1, 0, 0), perm(0, 0, 1), perm(0, 0, -1), perm(0, 1, 0)
CORE = [(g, g ^ 1) for g in range(4)]
ZHI = [(g, g ^ 2) for g in range(4)]


def send(array, pairs):
    return lax.ppermute(array, "blk", pairs)


def off_chip(array):
    return pltpu.with_memory_space_constraint(array, pltpu.HBM)


def vmem(count):
    return [pl.BlockSpec(memory_space=pltpu.VMEM)] * count


def params():
    return pltpu.CompilerParams(vmem_limit_bytes=LIMIT)


def pick_kernel(batches, amp_ref, out_ref, sems):
    g = lax.axis_index("grp")

    def copy(k):
        owner = g ^ (2 * (k & 1) + (k >> 2))
        at = batches[2 * owner + ((k >> 1) & 1)]
        src = amp_ref.at[:, pl.ds(pl.multiple_of(at * BATCH, BATCH), BATCH)]
        return pltpu.make_async_copy(src, out_ref.at[:, pl.ds(k * BATCH, BATCH)], sems.at[k])

    for k in range(NB):
        copy(k).start()
    for k in range(NB):
        copy(k).wait()


def pick(amplitudes, batches):
    return pl.pallas_call(
        pick_kernel,
        out_shape=jax.ShapeDtypeStruct(amplitudes.shape, BF16),
        grid_spec=pltpu.PrefetchScalarGridSpec(
            num_scalar_prefetch=1,
            grid=(),
            in_specs=[pl.BlockSpec(memory_space=pltpu.HBM)],
            out_specs=pl.BlockSpec(memory_space=pltpu.VMEM),
            scratch_shapes=[pltpu.SemaphoreType.DMA((NB,))],
        ),
        cost_estimate=pl.CostEstimate(flops=1000, bytes_accessed=1 << 20, transcendentals=0),
        compiler_params=params(),
        name="pick",
    )(batches, off_chip(amplitudes))


def keep_kernel(first, mask_ref, v_ref, out_ref, sems):
    tiles = out_ref.shape[0] // BLOCK

    def copy(r):
        rows = pl.ds((first + r) * BLOCK, BLOCK)
        return pltpu.make_async_copy(v_ref.at[rows], out_ref.at[pl.ds(r * BLOCK, BLOCK)], sems.at[r])

    for r in range(tiles):
        copy(r).start()
    for r in range(tiles):
        copy(r).wait()

        def body(c, carry, r=r):
            for k in range(8):
                at = pl.ds(pl.multiple_of((c * 8 + k) * BLOCK, BLOCK), BLOCK)
                tile = out_ref[r * BLOCK : (r + 1) * BLOCK, at]
                kept = mask_ref[first + r, c * 8 + k] != 0
                out_ref[r * BLOCK : (r + 1) * BLOCK, at] = jnp.where(kept, tile, jnp.zeros_like(tile))
            return carry

        lax.fori_loop(0, out_ref.shape[1] // (8 * BLOCK), body, 0)


def keep(first, tiles, v, mask):
    return pl.pallas_call(
        functools.partial(keep_kernel, first),
        out_shape=jax.ShapeDtypeStruct((tiles * BLOCK, v.shape[1]), BF16),
        grid_spec=pltpu.PrefetchScalarGridSpec(
            num_scalar_prefetch=1,
            grid=(),
            in_specs=[pl.BlockSpec(memory_space=pltpu.HBM)],
            out_specs=pl.BlockSpec(memory_space=pltpu.VMEM),
            scratch_shapes=[pltpu.SemaphoreType.DMA((tiles,))],
        ),
        cost_estimate=pl.CostEstimate(flops=1000, bytes_accessed=tiles << 21, transcendentals=0),
        compiler_params=params(),
    )(mask, off_chip(v))


def lay_kernel(slots, base, *refs):
    sources, outs = refs[: len(slots)], refs[-2:]
    for slot, source in zip(slots, sources):
        for k in range(2):
            at = base + 2 * BATCH * k
            outs[k][slot] = source[:, at : at + 2 * BATCH]


def lay(slots, base, arrays, before=()):
    out = jax.ShapeDtypeStruct((6, arrays[0].shape[0], 2 * BATCH), BF16)
    return pl.pallas_call(
        functools.partial(lay_kernel, slots, base),
        out_shape=(out, out),
        in_specs=vmem(len(arrays)) + [pl.BlockSpec(memory_space=pl.ANY)] * len(before),
        out_specs=vmem(2),
        input_output_aliases={len(arrays) + k: k for k in range(len(before))},
        cost_estimate=pl.CostEstimate(flops=1000, bytes_accessed=1 << 20, transcendentals=0),
        compiler_params=params(),
    )(*arrays, *before)


def dot(a, b):
    return jnp.dot(a, b, preferred_element_type=F32)


def column(offset):
    b = lax.axis_index("blk")
    x, z, y = b // (NZ * NY), (b // NY) % NZ, b % NY
    dx, dz, dy = offset
    at = ((x + dx) & 3) * (NZ * NY) + (z ^ dz) * NY + ((y + dy) & 3)
    return pl.ds(pl.multiple_of(at * 256, 256), 256)


def cross_kernel(offsets, *refs):
    steps = len(offsets)
    parts, (top, bottom), before, acc_ref = refs[:steps], refs[steps : steps + 2], refs[steps + 2 : -1], refs[-1]
    rows = top.shape[0]
    for i, offset in enumerate(offsets):
        for k, v_ref in enumerate((top, bottom)):
            at = slice(k * rows, (k + 1) * rows)
            product = dot(v_ref[:, column(offset)], parts[i][...])
            if i > 0:
                acc_ref[at, :] += product
            else:
                acc_ref[at, :] = before[0][at, :] + product if before else product


def cross(offsets, parts, v, before=()):
    rows = 2 * v[0].shape[0]
    steps = len(parts)
    return pl.pallas_call(
        functools.partial(cross_kernel, offsets),
        out_shape=jax.ShapeDtypeStruct((rows, NB * BATCH), F32),
        in_specs=vmem(steps + 2 + len(before)),
        out_specs=pl.BlockSpec(memory_space=pltpu.VMEM),
        cost_estimate=pl.CostEstimate(
            flops=2 * rows * steps * 256 * 1024, bytes_accessed=steps << 20, transcendentals=0
        ),
        compiler_params=params(),
    )(*parts, *v, *before)


def group_kernel(index, *refs):
    ys, xs, (top, bottom, acc_ref, mine, theirs) = refs[:3], refs[3:6], refs[6:]
    cols, rows = mine.shape[1], top.shape[0]
    for k, v_ref in enumerate((top, bottom)):
        at = slice(k * rows, (k + 1) * rows)
        first = True
        for j, dy in enumerate(LINE):
            for i, dx in enumerate(LINE):
                for dz in (0, 1):
                    tile = v_ref[:, column((dx, dz, dy))]
                    for out, part, slot, base in (
                        (mine, ys[j], 2 * i + dz, index),
                        (theirs, xs[i], 2 * j + dz, 2 + index),
                    ):
                        product = dot(tile, part[slot])
                        if first:
                            out[at, :] = acc_ref[at, base * cols : (base + 1) * cols] + product
                        else:
                            out[at, :] += product
                    first = False


def group(index, ys, xs, v, acc):
    rows = 2 * v[0].shape[0]
    cols = ys[0].shape[2]
    out = jax.ShapeDtypeStruct((rows, cols), F32)
    return pl.pallas_call(
        functools.partial(group_kernel, index),
        out_shape=(out, out),
        in_specs=vmem(9),
        out_specs=vmem(2),
        cost_estimate=pl.CostEstimate(
            flops=2 * rows * 18 * 256 * 512, bytes_accessed=18 << 20, transcendentals=0
        ),
        compiler_params=params(),
    )(*ys, *xs, *v, acc)


def finish_kernel(*refs):
    out_ref = refs[-1]
    for k in range(2):
        mine, got, far = refs[3 * k : 3 * k + 3]
        total = mine[:, :BATCH] + got[:, :BATCH] + far[...]
        out_ref[k * BATCH : (k + 1) * BATCH, :] = total.T.astype(BF16)


def finish(parts):
    rows = parts[0].shape[0]
    return pl.pallas_call(
        finish_kernel,
        out_shape=jax.ShapeDtypeStruct((2 * BATCH, rows), BF16),
        in_specs=vmem(6),
        out_specs=pl.BlockSpec(memory_space=pltpu.VMEM),
        cost_estimate=pl.CostEstimate(flops=1000000, bytes_accessed=3 << 20, transcendentals=0),
        compiler_params=params(),
        name="finish",
    )(*parts)


def on_device(integrals, block_mask, amplitudes, pair_batches):
    own = pick(amplitudes, pair_batches)
    near = send(own, ZX)
    xp0, yp0 = send(own, XM), send(own, YM)
    xm0, ym0 = send(own, XP), send(own, YP)
    xp1, yp1 = send(near, XM), send(near, YM)
    xm1, ym1 = send(near, XP), send(near, YP)
    x20, y20 = send(xm0, XP), send(ym0, YP)
    x21, y21 = send(xp1, XM), send(yp1, YM)

    early_x = lay((0, 1, 2, 3), 0, [xm0, xm1, xp0, xp1])
    early_y = lay((0, 1, 2, 3), 512, [ym0, ym1, yp0, yp1])
    along_x = lay((4, 5), 0, [x20, x21], early_x)
    along_y = lay((4, 5), 512, [y20, y21], early_y)

    pieces = []
    for k in range(2):
        ym, yp = send(along_x[k], YP), send(along_x[k], YM)
        xm, xp = send(along_y[k], XP), send(along_y[k], XM)
        if k == 0:
            y2, x2 = send(ym, YP), send(xm, XP)
        else:
            y2, x2 = send(yp, YM), send(xp, XM)
        pieces.append(([ym, yp, y2], [xm, xp, x2]))

    v = [keep(4 * k, 4, integrals, block_mask) for k in range(2)]
    near_at = [(-1, 0, 0), (1, 0, 0), (0, 0, -1), (0, 0, 1)]
    far_at = [(dx, 1, dy) for dx, dz, dy in near_at] + [(2, 0, 0), (2, 1, 0), (0, 0, 2), (0, 1, 2)]
    acc = cross([(0, 0, 0), (0, 1, 0)] + near_at, [own, near, xm0, xp0, ym0, yp0], v)
    acc = cross(far_at, [xm1, xp1, ym1, yp1, x20, x21, y20, y21], v, [acc])

    parts = []
    for k in range(2):
        mine, theirs = group(k, *pieces[k], v, acc)
        got = lax.ppermute(theirs, "grp", CORE)
        far = lax.ppermute(mine[:, BATCH:] + got[:, BATCH:], "grp", ZHI)
        parts += [mine, got, far]
    return finish(parts)


def solution(mesh):
    in_specs = (P("blk", "grp"), P("blk", "grp"), P(("grp", "blk"), None), P())
    out_specs = P("grp", "blk")

    return jax.shard_map(on_device, mesh=mesh, in_specs=in_specs, out_specs=out_specs, check_vma=False)
```

```python
import functools

import jax
import jax.numpy as jnp
from jax import lax
from jax.experimental import pallas as pl
from jax.experimental.pallas import tpu as pltpu
from jax.sharding import PartitionSpec as P


BLOCK = 128
BATCH = 128
NB = 8
NX, NZ, NY = 4, 2, 4
F32, BF16 = jnp.float32, jnp.bfloat16

LIMIT = 6 << 20
LINE = (-1, 1, 2)
TAIL = 64


def blk(x, z, y):
    return (x % NX) * (NZ * NY) + z * NY + y % NY


def perm(dx, dz, dy):
    cells = [(x, z, y) for x in range(NX) for z in range(NZ) for y in range(NY)]
    return [(blk(x, z, y), blk(x + dx, z ^ dz, y + dy)) for x, z, y in cells]


XP, XM, YP, YM, ZX = perm(1, 0, 0), perm(-1, 0, 0), perm(0, 0, 1), perm(0, 0, -1), perm(0, 1, 0)
CORE = [(g, g ^ 1) for g in range(4)]
ZHI = [(g, g ^ 2) for g in range(4)]


def send(array, pairs):
    return lax.ppermute(array, "blk", pairs)


def off_chip(array):
    return pltpu.with_memory_space_constraint(array, pltpu.HBM)


def vmem(count):
    return [pl.BlockSpec(memory_space=pltpu.VMEM)] * count


def params():
    return pltpu.CompilerParams(vmem_limit_bytes=LIMIT)


def pick_kernel(batches, amp_ref, out_ref, sems):
    g = lax.axis_index("grp")

    def copy(k):
        owner = g ^ (2 * (k & 1) + 1 - (k >> 2))
        at = batches[2 * owner + ((k >> 1) & 1)]
        src = amp_ref.at[:, pl.ds(pl.multiple_of(at * BATCH, BATCH), BATCH)]
        return pltpu.make_async_copy(src, out_ref.at[:, pl.ds(k * BATCH, BATCH)], sems.at[k])

    for k in range(NB):
        copy(k).start()
    for k in range(NB):
        copy(k).wait()


def pick(amplitudes, batches):
    return pl.pallas_call(
        pick_kernel,
        out_shape=jax.ShapeDtypeStruct(amplitudes.shape, BF16),
        grid_spec=pltpu.PrefetchScalarGridSpec(
            num_scalar_prefetch=1,
            grid=(),
            in_specs=[pl.BlockSpec(memory_space=pltpu.HBM)],
            out_specs=pl.BlockSpec(memory_space=pltpu.VMEM),
            scratch_shapes=[pltpu.SemaphoreType.DMA((NB,))],
        ),
        cost_estimate=pl.CostEstimate(flops=1000, bytes_accessed=1 << 20, transcendentals=0),
        compiler_params=params(),
        name="pick",
    )(batches, off_chip(amplitudes))


def keep_kernel(first, mask_ref, v_ref, out_ref, sems):
    tiles = out_ref.shape[0] // BLOCK

    def copy(r):
        rows = pl.ds((first + r) * BLOCK, BLOCK)
        return pltpu.make_async_copy(v_ref.at[rows], out_ref.at[pl.ds(r * BLOCK, BLOCK)], sems.at[r])

    for r in range(tiles):
        copy(r).start()
    for r in range(tiles):
        copy(r).wait()

        def body(c, carry, r=r):
            for k in range(8):
                at = pl.ds(pl.multiple_of((c * 8 + k) * BLOCK, BLOCK), BLOCK)
                tile = out_ref[r * BLOCK : (r + 1) * BLOCK, at]
                kept = mask_ref[first + r, c * 8 + k] != 0
                out_ref[r * BLOCK : (r + 1) * BLOCK, at] = jnp.where(kept, tile, jnp.zeros_like(tile))
            return carry

        lax.fori_loop(0, out_ref.shape[1] // (8 * BLOCK), body, 0)


def keep(first, tiles, v, mask):
    return pl.pallas_call(
        functools.partial(keep_kernel, first),
        out_shape=jax.ShapeDtypeStruct((tiles * BLOCK, v.shape[1]), BF16),
        grid_spec=pltpu.PrefetchScalarGridSpec(
            num_scalar_prefetch=1,
            grid=(),
            in_specs=[pl.BlockSpec(memory_space=pltpu.HBM)],
            out_specs=pl.BlockSpec(memory_space=pltpu.VMEM),
            scratch_shapes=[pltpu.SemaphoreType.DMA((tiles,))],
        ),
        cost_estimate=pl.CostEstimate(flops=1000, bytes_accessed=tiles << 21, transcendentals=0),
        compiler_params=params(),
    )(mask, off_chip(v))


def lay_kernel(slots, base, *refs):
    sources, outs = refs[: len(slots)], refs[-2:]
    for slot, source in zip(slots, sources):
        for k in range(2):
            at = base + 2 * BATCH * k
            outs[k][slot] = source[:, at : at + 2 * BATCH]


def lay(slots, base, arrays, before=()):
    out = jax.ShapeDtypeStruct((6, arrays[0].shape[0], 2 * BATCH), BF16)
    return pl.pallas_call(
        functools.partial(lay_kernel, slots, base),
        out_shape=(out, out),
        in_specs=vmem(len(arrays)) + [pl.BlockSpec(memory_space=pl.ANY)] * len(before),
        out_specs=vmem(2),
        input_output_aliases={len(arrays) + k: k for k in range(len(before))},
        cost_estimate=pl.CostEstimate(flops=1000, bytes_accessed=1 << 20, transcendentals=0),
        compiler_params=params(),
    )(*arrays, *before)


def dot(a, b):
    return jnp.dot(a, b, preferred_element_type=F32)


def column(offset):
    b = lax.axis_index("blk")
    x, z, y = b // (NZ * NY), (b // NY) % NZ, b % NY
    dx, dz, dy = offset
    at = ((x + dx) & 3) * (NZ * NY) + (z ^ dz) * NY + ((y + dy) & 3)
    return pl.ds(pl.multiple_of(at * 256, 256), 256)


def cross_kernel(offsets, *refs):
    steps = len(offsets)
    parts, (top, bottom), before, acc_ref = refs[:steps], refs[steps : steps + 2], refs[steps + 2 : -1], refs[-1]
    rows = top.shape[0]
    for i, offset in enumerate(offsets):
        for k, v_ref in enumerate((top, bottom)):
            at = slice(k * rows, (k + 1) * rows)
            product = dot(v_ref[:, column(offset)], parts[i][...])
            if i > 0:
                acc_ref[at, :] += product
            else:
                acc_ref[at, :] = before[0][at, :] + product if before else product


def cross(offsets, parts, v, before=()):
    rows = 2 * v[0].shape[0]
    steps = len(parts)
    return pl.pallas_call(
        functools.partial(cross_kernel, offsets),
        out_shape=jax.ShapeDtypeStruct((rows, NB * BATCH), F32),
        in_specs=vmem(steps + 2 + len(before)),
        out_specs=pl.BlockSpec(memory_space=pltpu.VMEM),
        cost_estimate=pl.CostEstimate(
            flops=2 * rows * steps * 256 * 1024, bytes_accessed=steps << 20, transcendentals=0
        ),
        compiler_params=params(),
    )(*parts, *v, *before)


def group_kernel(base, turned, *refs):
    parts, (top, bottom, acc_ref, out) = refs[:3], refs[3:]
    cols, rows = out.shape[1], top.shape[0]
    for k, v_ref in enumerate((top, bottom)):
        at = slice(k * rows, (k + 1) * rows)
        first = True
        for j, far in enumerate(LINE):
            for i, near in enumerate(LINE):
                for dz in (0, 1):
                    offset = (far, dz, near) if turned else (near, dz, far)
                    product = dot(v_ref[:, column(offset)], parts[j][2 * i + dz])
                    if first:
                        out[at, :] = acc_ref[at, base * cols : (base + 1) * cols] + product
                    else:
                        out[at, :] += product
                    first = False


def group(base, turned, parts, v, acc):
    rows = 2 * v[0].shape[0]
    cols = parts[0].shape[2]
    return pl.pallas_call(
        functools.partial(group_kernel, base, turned),
        out_shape=jax.ShapeDtypeStruct((rows, cols), F32),
        in_specs=vmem(6),
        out_specs=pl.BlockSpec(memory_space=pltpu.VMEM),
        cost_estimate=pl.CostEstimate(
            flops=2 * rows * 18 * 256 * 256, bytes_accessed=18 << 19, transcendentals=0
        ),
        compiler_params=params(),
    )(*parts, *v, acc)


def code_kernel(mine, got, out_ref):
    rows = mine.shape[0]
    powers = []
    for r in range(rows // BLOCK):
        at = slice(r * BLOCK, (r + 1) * BLOCK)
        total = mine[at, BATCH:] + got[at, BATCH:]
        peak = jnp.maximum(jnp.max(jnp.abs(total), axis=0, keepdims=True), 1e-30)
        power = jnp.floor(jnp.log2(peak * 1.0001)) - 14.0
        scaled = jnp.clip(jnp.round(total * jnp.exp2(-power)), -32767.0, 32767.0)
        out_ref[at, :] = scaled.astype(jnp.int32).astype(jnp.int16)
        powers.append(jnp.broadcast_to(power, (TAIL // 8, BATCH)))
    out_ref[rows:, :] = jnp.concatenate(powers, axis=0).astype(jnp.int32).astype(jnp.int16)


def code(mine, got):
    return pl.pallas_call(
        code_kernel,
        out_shape=jax.ShapeDtypeStruct((mine.shape[0] + TAIL, BATCH), jnp.int16),
        in_specs=vmem(2),
        out_specs=pl.BlockSpec(memory_space=pltpu.VMEM),
        cost_estimate=pl.CostEstimate(flops=1000, bytes_accessed=1 << 20, transcendentals=0),
        compiler_params=params(),
        name="code",
    )(mine, got)


def finish_kernel(*refs):
    out_ref = refs[-1]
    for k in range(2):
        mine, got, far = refs[3 * k : 3 * k + 3]
        rows = mine.shape[0]
        powers = far[rows:, :].astype(jnp.int32).astype(F32)
        for r in range(rows // BLOCK):
            at = slice(r * BLOCK, (r + 1) * BLOCK)
            scale = jnp.exp2(powers[r * (TAIL // 8) : r * (TAIL // 8) + 1])
            other = far[at, :].astype(jnp.int32).astype(F32) * scale
            total = mine[at, :BATCH] + got[at, :BATCH] + other
            out_ref[k * BATCH : (k + 1) * BATCH, at] = total.T.astype(BF16)


def finish(parts):
    rows = parts[0].shape[0]
    return pl.pallas_call(
        finish_kernel,
        out_shape=jax.ShapeDtypeStruct((2 * BATCH, rows), BF16),
        in_specs=vmem(6),
        out_specs=pl.BlockSpec(memory_space=pltpu.VMEM),
        cost_estimate=pl.CostEstimate(flops=1000000, bytes_accessed=3 << 20, transcendentals=0),
        compiler_params=params(),
        name="finish",
    )(*parts)


def on_device(integrals, block_mask, amplitudes, pair_batches):
    own = pick(amplitudes, pair_batches)
    near = send(own, ZX)
    xp0, yp0 = send(own, XM), send(own, YM)
    xm0, ym0 = send(own, XP), send(own, YP)
    xp1, yp1 = send(near, XM), send(near, YM)
    xm1, ym1 = send(near, XP), send(near, YP)
    x20, y20 = send(xm0, XP), send(ym0, YP)
    x21, y21 = send(xp1, XM), send(yp1, YM)

    early_x = lay((0, 1, 2, 3), 0, [xm0, xm1, xp0, xp1])
    early_y = lay((0, 1, 2, 3), 512, [ym0, ym1, yp0, yp1])
    along_x = lay((4, 5), 0, [x20, x21], early_x)
    along_y = lay((4, 5), 512, [y20, y21], early_y)

    pieces = []
    for k in range(2):
        ym, yp = send(along_x[k], YP), send(along_x[k], YM)
        xm, xp = send(along_y[k], XP), send(along_y[k], XM)
        if k == 0:
            y2, x2 = send(ym, YP), send(xm, XP)
        else:
            y2, x2 = send(yp, YM), send(xp, XM)
        pieces.append(([ym, yp, y2], [xm, xp, x2]))

    v = [keep(4 * k, 4, integrals, block_mask) for k in range(2)]
    near_at = [(-1, 0, 0), (1, 0, 0), (0, 0, -1), (0, 0, 1)]
    far_at = [(dx, 1, dy) for dx, dz, dy in near_at] + [(2, 0, 0), (2, 1, 0), (0, 0, 2), (0, 1, 2)]
    acc = cross([(0, 0, 0), (0, 1, 0)] + near_at, [own, near, xm0, xp0, ym0, yp0], v)
    acc = cross(far_at, [xm1, xp1, ym1, yp1, x20, x21, y20, y21], v, [acc])

    parts = []
    for k in range(2):
        ys, xs = pieces[k]
        theirs = group(k, False, ys, v, acc)
        got = lax.ppermute(theirs, "grp", CORE)
        mine = group(2 + k, True, xs, v, acc)
        packed = code(mine, got)
        far = lax.ppermute(packed, "grp", ZHI)
        parts += [mine, got, far]
    return finish(parts)


def solution(mesh):
    in_specs = (P("blk", "grp"), P("blk", "grp"), P(("grp", "blk"), None), P())
    out_specs = P("grp", "blk")

    return jax.shard_map(on_device, mesh=mesh, in_specs=in_specs, out_specs=out_specs, check_vma=False)
```

```python
import functools

import jax
import jax.numpy as jnp
from jax import lax
from jax.experimental import pallas as pl
from jax.experimental.pallas import tpu as pltpu
from jax.sharding import PartitionSpec as P


BLOCK = 128
BATCH = 128
NB = 8
NX, NZ, NY = 4, 2, 4
F32, BF16 = jnp.float32, jnp.bfloat16

LIMIT = 6 << 20
LINE = (-1, 1, 2)
TAIL = 64
HALF = 512


def blk(x, z, y):
    return (x % NX) * (NZ * NY) + z * NY + y % NY


def perm(dx, dz, dy):
    cells = [(x, z, y) for x in range(NX) for z in range(NZ) for y in range(NY)]
    return [(blk(x, z, y), blk(x + dx, z ^ dz, y + dy)) for x, z, y in cells]


XP, XM, YP, YM, ZX = perm(1, 0, 0), perm(-1, 0, 0), perm(0, 0, 1), perm(0, 0, -1), perm(0, 1, 0)
CORE = [(g, g ^ 1) for g in range(4)]
ZHI = [(g, g ^ 2) for g in range(4)]


def send(array, pairs):
    return lax.ppermute(array, "blk", pairs)


def off_chip(array):
    return pltpu.with_memory_space_constraint(array, pltpu.HBM)


def vmem(count):
    return [pl.BlockSpec(memory_space=pltpu.VMEM)] * count


def params():
    return pltpu.CompilerParams(vmem_limit_bytes=LIMIT)


def pick_kernel(batches, amp_ref, out_ref, sems):
    g = lax.axis_index("grp")

    def copy(k):
        owner = g ^ (2 * (k & 1) + 1 - (k >> 2))
        at = batches[2 * owner + ((k >> 1) & 1)]
        src = amp_ref.at[:, pl.ds(pl.multiple_of(at * BATCH, BATCH), BATCH)]
        return pltpu.make_async_copy(src, out_ref.at[:, pl.ds(k * BATCH, BATCH)], sems.at[k])

    for k in range(NB):
        copy(k).start()
    for k in range(NB):
        copy(k).wait()


def pick(amplitudes, batches):
    return pl.pallas_call(
        pick_kernel,
        out_shape=jax.ShapeDtypeStruct(amplitudes.shape, BF16),
        grid_spec=pltpu.PrefetchScalarGridSpec(
            num_scalar_prefetch=1,
            grid=(),
            in_specs=[pl.BlockSpec(memory_space=pltpu.HBM)],
            out_specs=pl.BlockSpec(memory_space=pltpu.VMEM),
            scratch_shapes=[pltpu.SemaphoreType.DMA((NB,))],
        ),
        cost_estimate=pl.CostEstimate(flops=1000, bytes_accessed=1 << 20, transcendentals=0),
        compiler_params=params(),
        name="pick",
    )(off_chip(batches), off_chip(amplitudes))


def keep_kernel(first, mask_ref, v_ref, out_ref, sems):
    tiles = out_ref.shape[0] // BLOCK

    def copy(r):
        rows = pl.ds((first + r) * BLOCK, BLOCK)
        return pltpu.make_async_copy(v_ref.at[rows], out_ref.at[pl.ds(r * BLOCK, BLOCK)], sems.at[r])

    for r in range(tiles):
        copy(r).start()
    for r in range(tiles):
        copy(r).wait()

        def body(c, carry, r=r):
            for k in range(8):
                at = pl.ds(pl.multiple_of((c * 8 + k) * BLOCK, BLOCK), BLOCK)
                tile = out_ref[r * BLOCK : (r + 1) * BLOCK, at]
                kept = mask_ref[first + r, c * 8 + k] != 0
                out_ref[r * BLOCK : (r + 1) * BLOCK, at] = jnp.where(kept, tile, jnp.zeros_like(tile))
            return carry

        lax.fori_loop(0, out_ref.shape[1] // (8 * BLOCK), body, 0)


def keep(first, tiles, v, mask):
    return pl.pallas_call(
        functools.partial(keep_kernel, first),
        out_shape=jax.ShapeDtypeStruct((tiles * BLOCK, v.shape[1]), BF16),
        grid_spec=pltpu.PrefetchScalarGridSpec(
            num_scalar_prefetch=1,
            grid=(),
            in_specs=[pl.BlockSpec(memory_space=pltpu.HBM)],
            out_specs=pl.BlockSpec(memory_space=pltpu.VMEM),
            scratch_shapes=[pltpu.SemaphoreType.DMA((tiles,))],
        ),
        cost_estimate=pl.CostEstimate(flops=1000, bytes_accessed=tiles << 21, transcendentals=0),
        compiler_params=params(),
    )(off_chip(mask), off_chip(v))


def lay_kernel(slots, base, *refs):
    sources, outs = refs[: len(slots)], refs[-2:]
    for slot, source in zip(slots, sources):
        for k in range(2):
            at = 2 * BATCH * k + (base if source.shape[1] > HALF else 0)
            outs[k][slot] = source[:, at : at + 2 * BATCH]


def lay(slots, base, arrays, before=()):
    out = jax.ShapeDtypeStruct((6, arrays[0].shape[0], 2 * BATCH), BF16)
    return pl.pallas_call(
        functools.partial(lay_kernel, slots, base),
        out_shape=(out, out),
        in_specs=vmem(len(arrays)) + [pl.BlockSpec(memory_space=pl.ANY)] * len(before),
        out_specs=vmem(2),
        input_output_aliases={len(arrays) + k: k for k in range(len(before))},
        cost_estimate=pl.CostEstimate(flops=1000, bytes_accessed=1 << 20, transcendentals=0),
        compiler_params=params(),
    )(*arrays, *before)


def halves_kernel(plan, *refs):
    outs = refs[-len(plan) :]
    for out, places in zip(outs, plan):
        for k, (i, base) in enumerate(places):
            piece = refs[i][:, base : base + HALF]
            if len(places) == 1:
                out[...] = piece
            else:
                out[k] = piece


def halves(plan, arrays):
    rows = arrays[0].shape[0]
    lead = [() if len(places) == 1 else (len(places),) for places in plan]
    return pl.pallas_call(
        functools.partial(halves_kernel, plan),
        out_shape=[jax.ShapeDtypeStruct(n + (rows, HALF), BF16) for n in lead],
        in_specs=vmem(len(arrays)),
        out_specs=vmem(len(plan)),
        cost_estimate=pl.CostEstimate(flops=1000, bytes_accessed=1 << 20, transcendentals=0),
        compiler_params=params(),
    )(*arrays)


def dot(a, b):
    return jnp.dot(a, b, preferred_element_type=F32)


def column(offset):
    b = lax.axis_index("blk")
    x, z, y = b // (NZ * NY), (b // NY) % NZ, b % NY
    dx, dz, dy = offset
    at = ((x + dx) & 3) * (NZ * NY) + (z ^ dz) * NY + ((y + dy) & 3)
    return pl.ds(pl.multiple_of(at * 256, 256), 256)


def cross_kernel(offsets, picks, n_arrays, *refs):
    arrays, (top, bottom), before, acc_ref = (
        refs[:n_arrays],
        refs[n_arrays : n_arrays + 2],
        refs[n_arrays + 2 : -1],
        refs[-1],
    )
    rows = top.shape[0]
    for step, (offset, parts) in enumerate(zip(offsets, picks)):
        width = acc_ref.shape[1] // len(parts)
        for k, v_ref in enumerate((top, bottom)):
            at = slice(k * rows, (k + 1) * rows)
            tile = v_ref[:, column(offset)]
            for h, (i, slot) in enumerate(parts):
                cols = slice(h * width, (h + 1) * width)
                product = dot(tile, arrays[i][...] if slot is None else arrays[i][slot])
                if step > 0:
                    acc_ref[at, cols] += product
                else:
                    acc_ref[at, cols] = before[0][at, cols] + product if before else product


def cross(offsets, picks, arrays, v, before=()):
    rows = 2 * v[0].shape[0]
    steps = len(offsets)
    return pl.pallas_call(
        functools.partial(cross_kernel, offsets, picks, len(arrays)),
        out_shape=jax.ShapeDtypeStruct((rows, NB * BATCH), F32),
        in_specs=vmem(len(arrays) + 2 + len(before)),
        out_specs=pl.BlockSpec(memory_space=pltpu.VMEM),
        cost_estimate=pl.CostEstimate(
            flops=2 * rows * steps * 256 * 1024, bytes_accessed=steps << 20, transcendentals=0
        ),
        compiler_params=params(),
    )(*arrays, *v, *before)


def group_kernel(base, turned, fars, *refs):
    parts, (top, bottom, acc_ref, out) = refs[: len(fars)], refs[len(fars) :]
    cols, rows = out.shape[1], top.shape[0]
    for k, v_ref in enumerate((top, bottom)):
        at = slice(k * rows, (k + 1) * rows)
        first = True
        for j, far in enumerate(fars):
            for i, near in enumerate(LINE):
                for dz in (0, 1):
                    offset = (far, dz, near) if turned else (near, dz, far)
                    product = dot(v_ref[:, column(offset)], parts[j][2 * i + dz])
                    if first:
                        out[at, :] = acc_ref[at, base * cols : (base + 1) * cols] + product
                    else:
                        out[at, :] += product
                    first = False


def group(base, turned, fars, parts, v, acc):
    rows = 2 * v[0].shape[0]
    cols = parts[0].shape[2]
    return pl.pallas_call(
        functools.partial(group_kernel, base, turned, fars),
        out_shape=jax.ShapeDtypeStruct((rows, cols), F32),
        in_specs=vmem(len(parts) + 3),
        out_specs=pl.BlockSpec(memory_space=pltpu.VMEM),
        cost_estimate=pl.CostEstimate(
            flops=2 * rows * 6 * len(parts) * 256 * 256, bytes_accessed=18 << 19, transcendentals=0
        ),
        compiler_params=params(),
    )(*parts, *v, acc)


def code_kernel(mine, got, out_ref):
    rows = mine.shape[0]
    powers = []
    for r in range(rows // BLOCK):
        at = slice(r * BLOCK, (r + 1) * BLOCK)
        total = mine[at, BATCH:] + got[at, BATCH:]
        peak = jnp.maximum(jnp.max(jnp.abs(total), axis=0, keepdims=True), 1e-30)
        power = jnp.floor(jnp.log2(peak * 1.0001)) - 14.0
        scaled = jnp.clip(jnp.round(total * jnp.exp2(-power)), -32767.0, 32767.0)
        out_ref[at, :] = scaled.astype(jnp.int32).astype(jnp.int16)
        powers.append(jnp.broadcast_to(power, (TAIL // 8, BATCH)))
    out_ref[rows:, :] = jnp.concatenate(powers, axis=0).astype(jnp.int32).astype(jnp.int16)


def code(mine, got):
    return pl.pallas_call(
        code_kernel,
        out_shape=jax.ShapeDtypeStruct((mine.shape[0] + TAIL, BATCH), jnp.int16),
        in_specs=vmem(2),
        out_specs=pl.BlockSpec(memory_space=pltpu.VMEM),
        cost_estimate=pl.CostEstimate(flops=1000, bytes_accessed=1 << 20, transcendentals=0),
        compiler_params=params(),
        name="code",
    )(mine, got)


def finish_kernel(*refs):
    out_ref = refs[-1]
    for k in range(2):
        mine, got, far = refs[3 * k : 3 * k + 3]
        rows = mine.shape[0]
        powers = far[rows:, :].astype(jnp.int32).astype(F32)
        for r in range(rows // BLOCK):
            at = slice(r * BLOCK, (r + 1) * BLOCK)
            scale = jnp.exp2(powers[r * (TAIL // 8) : r * (TAIL // 8) + 1])
            other = far[at, :].astype(jnp.int32).astype(F32) * scale
            total = mine[at, :BATCH] + got[at, :BATCH] + other
            out_ref[k * BATCH : (k + 1) * BATCH, at] = total.T.astype(BF16)


def finish(parts):
    rows = parts[0].shape[0]
    return pl.pallas_call(
        finish_kernel,
        out_shape=jax.ShapeDtypeStruct((2 * BATCH, rows), BF16),
        in_specs=vmem(6),
        out_specs=pl.BlockSpec(memory_space=pltpu.VMEM),
        cost_estimate=pl.CostEstimate(flops=1000000, bytes_accessed=3 << 20, transcendentals=0),
        compiler_params=params(),
        name="finish",
    )(*parts)


def on_device(integrals, block_mask, amplitudes, pair_batches):
    own = pick(amplitudes, pair_batches)
    near = send(own, ZX)
    xp0, yp0 = send(own, XM), send(own, YM)
    xm0, ym0 = send(own, XP), send(own, YP)
    near_a, near_b = halves([[(0, 0)], [(0, HALF)]], [near])
    xp1, yp1 = send(near_a, XM), send(near_b, YM)
    xm1, ym1 = send(near_a, XP), send(near_b, YP)
    plan = [[(0, 0)], [(1, HALF)], [(0, HALF)], [(1, 0)], [(0, HALF), (2, HALF)], [(1, 0), (3, 0)]]
    xa, yb, xb, ya, zx, zy = halves(plan, [xm0, ym0, xp0, yp0])
    x20, y20 = send(xa, XP), send(yb, YP)
    x21, y21 = send(xp1, XM), send(yp1, YM)
    x20b, y20a = send(xb, XP), send(ya, YP)
    zx, zy = send(zx, ZX), send(zy, ZX)
    zd = send(halves([[(0, 0), (1, 0)]], [x20b, y20a])[0], ZX)

    early_x = lay((0, 1, 2, 3), 0, [xm0, xm1, xp0, xp1])
    early_y = lay((0, 1, 2, 3), HALF, [ym0, ym1, yp0, yp1])
    along_x = lay((4, 5), 0, [x20, x21], early_x)
    along_y = lay((4, 5), HALF, [y20, y21], early_y)

    pieces = []
    for k in range(2):
        ym, yp = send(along_x[k], YP), send(along_x[k], YM)
        xm, xp = send(along_y[k], XP), send(along_y[k], XM)
        if k == 0:
            y2, x2 = send(ym, YP), send(xm, XP)
        else:
            y2, x2 = send(yp, YM), send(xp, XM)
        pieces.append(([ym, yp, y2], [xm, xp, x2]))

    v = [keep(4 * k, 4, integrals, block_mask) for k in range(2)]
    near_at = [(0, 0, 0), (0, 1, 0), (-1, 0, 0), (1, 0, 0), (0, 0, -1), (0, 0, 1)]
    arrays = [own, near, xm0, xp0, ym0, yp0]
    acc = cross(near_at, [[(i, None)] for i in range(6)], arrays, v)
    far_at = [(-1, 1, 0), (1, 1, 0), (0, 1, -1), (0, 1, 1), (2, 0, 0), (2, 1, 0), (0, 0, 2), (0, 1, 2)]
    arrays = [zx, zy, zd, xm1, xp1, ym1, yp1, x20, x20b, x21, y20a, y20, y21]
    picks = [
        [(3, None), (0, 0)],
        [(4, None), (0, 1)],
        [(1, 0), (5, None)],
        [(1, 1), (6, None)],
        [(7, None), (8, None)],
        [(9, None), (2, 0)],
        [(10, None), (11, None)],
        [(2, 1), (12, None)],
    ]
    acc = cross(far_at, picks, arrays, v, [acc])

    parts = []
    for k in range(2):
        ys, xs = pieces[k]
        if k == 0:
            theirs = group(0, False, LINE, ys, v, acc)
        else:
            begun = group(1, False, (1,), ys[1:2], v, acc)
            theirs = group(0, False, (-1, 2), ys[::2], v, begun)
        got = lax.ppermute(theirs, "grp", CORE)
        if k == 0:
            mine = group(2, True, LINE, xs, v, acc)
        else:
            begun = group(3, True, (1,), xs[1:2], v, acc)
            mine = group(0, True, (-1, 2), xs[::2], v, begun)
        packed = code(mine, got)
        far = lax.ppermute(packed, "grp", ZHI)
        parts += [mine, got, far]
    return finish(parts)


def solution(mesh):
    in_specs = (P("blk", "grp"), P("blk", "grp"), P(("grp", "blk"), None), P())
    out_specs = P("grp", "blk")

    return jax.shard_map(on_device, mesh=mesh, in_specs=in_specs, out_specs=out_specs, check_vma=False)
```

```python
import functools

import jax
import jax.numpy as jnp
from jax import lax
from jax.experimental import pallas as pl
from jax.experimental.pallas import tpu as pltpu
from jax.sharding import PartitionSpec as P


BLOCK = 128
BATCH = 128
NB = 8
NX, NZ, NY = 4, 2, 4
F32, BF16 = jnp.float32, jnp.bfloat16

LIMIT = 6 << 20
LINE = (-1, 1, 2)
TAIL = 64
HALF = 512


def blk(x, z, y):
    return (x % NX) * (NZ * NY) + z * NY + y % NY


def perm(dx, dz, dy):
    cells = [(x, z, y) for x in range(NX) for z in range(NZ) for y in range(NY)]
    return [(blk(x, z, y), blk(x + dx, z ^ dz, y + dy)) for x, z, y in cells]


XP, XM, YP, YM, ZX = perm(1, 0, 0), perm(-1, 0, 0), perm(0, 0, 1), perm(0, 0, -1), perm(0, 1, 0)
CORE = [(g, g ^ 1) for g in range(4)]
ZHI = [(g, g ^ 2) for g in range(4)]


def send(array, pairs):
    return lax.ppermute(array, "blk", pairs)


def off_chip(array):
    return pltpu.with_memory_space_constraint(array, pltpu.HBM)


def vmem(count):
    return [pl.BlockSpec(memory_space=pltpu.VMEM)] * count


def params():
    return pltpu.CompilerParams(vmem_limit_bytes=LIMIT)


def pick_kernel(batches, amp_ref, out_ref, sems):
    g = lax.axis_index("grp")

    def copy(k):
        owner = g ^ (2 * (k & 1) + 1 - (k >> 2))
        at = batches[2 * owner + ((k >> 1) & 1)]
        src = amp_ref.at[:, pl.ds(pl.multiple_of(at * BATCH, BATCH), BATCH)]
        return pltpu.make_async_copy(src, out_ref.at[:, pl.ds(k * BATCH, BATCH)], sems.at[k])

    for k in range(NB):
        copy(k).start()
    for k in range(NB):
        copy(k).wait()


def pick(amplitudes, batches):
    return pl.pallas_call(
        pick_kernel,
        out_shape=jax.ShapeDtypeStruct(amplitudes.shape, BF16),
        grid_spec=pltpu.PrefetchScalarGridSpec(
            num_scalar_prefetch=1,
            grid=(),
            in_specs=[pl.BlockSpec(memory_space=pltpu.HBM)],
            out_specs=pl.BlockSpec(memory_space=pltpu.VMEM),
            scratch_shapes=[pltpu.SemaphoreType.DMA((NB,))],
        ),
        cost_estimate=pl.CostEstimate(flops=1000, bytes_accessed=1 << 20, transcendentals=0),
        compiler_params=params(),
        name="pick",
    )(off_chip(batches), off_chip(amplitudes))


def keep_kernel(first, mask_ref, v_ref, out_ref, sems):
    tiles = out_ref.shape[0] // BLOCK

    def copy(r):
        rows = pl.ds((first + r) * BLOCK, BLOCK)
        return pltpu.make_async_copy(v_ref.at[rows], out_ref.at[pl.ds(r * BLOCK, BLOCK)], sems.at[r])

    for r in range(tiles):
        copy(r).start()
    for r in range(tiles):
        copy(r).wait()

        def body(c, carry, r=r):
            for k in range(8):
                at = pl.ds(pl.multiple_of((c * 8 + k) * BLOCK, BLOCK), BLOCK)
                tile = out_ref[r * BLOCK : (r + 1) * BLOCK, at]
                kept = mask_ref[first + r, c * 8 + k] != 0
                out_ref[r * BLOCK : (r + 1) * BLOCK, at] = jnp.where(kept, tile, jnp.zeros_like(tile))
            return carry

        lax.fori_loop(0, out_ref.shape[1] // (8 * BLOCK), body, 0)


def keep(first, tiles, v, mask):
    return pl.pallas_call(
        functools.partial(keep_kernel, first),
        out_shape=jax.ShapeDtypeStruct((tiles * BLOCK, v.shape[1]), BF16),
        grid_spec=pltpu.PrefetchScalarGridSpec(
            num_scalar_prefetch=1,
            grid=(),
            in_specs=[pl.BlockSpec(memory_space=pltpu.HBM)],
            out_specs=pl.BlockSpec(memory_space=pltpu.VMEM),
            scratch_shapes=[pltpu.SemaphoreType.DMA((tiles,))],
        ),
        cost_estimate=pl.CostEstimate(flops=1000, bytes_accessed=tiles << 21, transcendentals=0),
        compiler_params=params(),
    )(off_chip(mask), off_chip(v))


def lay_kernel(slots, base, *refs):
    sources, outs = refs[: len(slots)], refs[-2:]
    for slot, source in zip(slots, sources):
        for k in range(2):
            at = 2 * BATCH * k + (base if source.shape[1] > HALF else 0)
            outs[k][slot] = source[:, at : at + 2 * BATCH]


def lay(slots, base, arrays, before=()):
    out = jax.ShapeDtypeStruct((6, arrays[0].shape[0], 2 * BATCH), BF16)
    return pl.pallas_call(
        functools.partial(lay_kernel, slots, base),
        out_shape=(out, out),
        in_specs=vmem(len(arrays)) + [pl.BlockSpec(memory_space=pl.ANY)] * len(before),
        out_specs=vmem(2),
        input_output_aliases={len(arrays) + k: k for k in range(len(before))},
        cost_estimate=pl.CostEstimate(flops=1000, bytes_accessed=1 << 20, transcendentals=0),
        compiler_params=params(),
    )(*arrays, *before)


def halves_kernel(plan, *refs):
    outs = refs[-len(plan) :]
    for out, places in zip(outs, plan):
        for k, (i, base) in enumerate(places):
            piece = refs[i][:, base : base + HALF]
            if len(places) == 1:
                out[...] = piece
            else:
                out[k] = piece


def halves(plan, arrays):
    rows = arrays[0].shape[0]
    lead = [() if len(places) == 1 else (len(places),) for places in plan]
    return pl.pallas_call(
        functools.partial(halves_kernel, plan),
        out_shape=[jax.ShapeDtypeStruct(n + (rows, HALF), BF16) for n in lead],
        in_specs=vmem(len(arrays)),
        out_specs=vmem(len(plan)),
        cost_estimate=pl.CostEstimate(flops=1000, bytes_accessed=1 << 20, transcendentals=0),
        compiler_params=params(),
    )(*arrays)


def dot(a, b):
    return jnp.dot(a, b, preferred_element_type=F32)


def column(offset):
    b = lax.axis_index("blk")
    x, z, y = b // (NZ * NY), (b // NY) % NZ, b % NY
    dx, dz, dy = offset
    at = ((x + dx) & 3) * (NZ * NY) + (z ^ dz) * NY + ((y + dy) & 3)
    return pl.ds(pl.multiple_of(at * 256, 256), 256)


def cross_kernel(offsets, picks, n_arrays, *refs):
    arrays, (top, bottom), before, acc_ref = (
        refs[:n_arrays],
        refs[n_arrays : n_arrays + 2],
        refs[n_arrays + 2 : -1],
        refs[-1],
    )
    rows = top.shape[0]
    for step, (offset, parts) in enumerate(zip(offsets, picks)):
        width = acc_ref.shape[1] // len(parts)
        for k, v_ref in enumerate((top, bottom)):
            at = slice(k * rows, (k + 1) * rows)
            tile = v_ref[:, column(offset)]
            for h, (i, slot) in enumerate(parts):
                cols = slice(h * width, (h + 1) * width)
                product = dot(tile, arrays[i][...] if slot is None else arrays[i][slot])
                if step > 0:
                    acc_ref[at, cols] += product
                else:
                    acc_ref[at, cols] = before[0][at, cols] + product if before else product


def cross(offsets, picks, arrays, v, before=()):
    rows = 2 * v[0].shape[0]
    steps = len(offsets)
    return pl.pallas_call(
        functools.partial(cross_kernel, offsets, picks, len(arrays)),
        out_shape=jax.ShapeDtypeStruct((rows, NB * BATCH), F32),
        in_specs=vmem(len(arrays) + 2 + len(before)),
        out_specs=pl.BlockSpec(memory_space=pltpu.VMEM),
        cost_estimate=pl.CostEstimate(
            flops=2 * rows * steps * 256 * 1024, bytes_accessed=steps << 20, transcendentals=0
        ),
        compiler_params=params(),
    )(*arrays, *v, *before)


def group_kernel(base, turned, fars, *refs):
    parts, (top, bottom, acc_ref, out) = refs[: len(fars)], refs[len(fars) :]
    cols, rows = out.shape[1], top.shape[0]
    for k, v_ref in enumerate((top, bottom)):
        at = slice(k * rows, (k + 1) * rows)
        first = True
        for j, far in enumerate(fars):
            for i, near in enumerate(LINE):
                for dz in (0, 1):
                    offset = (far, dz, near) if turned else (near, dz, far)
                    product = dot(v_ref[:, column(offset)], parts[j][2 * i + dz])
                    if first:
                        out[at, :] = acc_ref[at, base * cols : (base + 1) * cols] + product
                    else:
                        out[at, :] += product
                    first = False


def group(base, turned, fars, parts, v, acc):
    rows = 2 * v[0].shape[0]
    cols = parts[0].shape[2]
    return pl.pallas_call(
        functools.partial(group_kernel, base, turned, fars),
        out_shape=jax.ShapeDtypeStruct((rows, cols), F32),
        in_specs=vmem(len(parts) + 3),
        out_specs=pl.BlockSpec(memory_space=pltpu.VMEM),
        cost_estimate=pl.CostEstimate(
            flops=2 * rows * 6 * len(parts) * 256 * 256, bytes_accessed=18 << 19, transcendentals=0
        ),
        compiler_params=params(),
    )(*parts, *v, acc)


def code_kernel(mine, got, out_ref):
    rows = mine.shape[0]
    powers = []
    for r in range(rows // BLOCK):
        at = slice(r * BLOCK, (r + 1) * BLOCK)
        total = mine[at, BATCH:] + got[at, BATCH:]
        peak = jnp.maximum(jnp.max(jnp.abs(total), axis=0, keepdims=True), 1e-30)
        power = jnp.floor(jnp.log2(peak * 1.0001)) - 14.0
        scaled = jnp.clip(jnp.round(total * jnp.exp2(-power)), -32767.0, 32767.0)
        out_ref[at, :] = scaled.astype(jnp.int32).astype(jnp.int16)
        powers.append(jnp.broadcast_to(power, (TAIL // 8, BATCH)))
    out_ref[rows:, :] = jnp.concatenate(powers, axis=0).astype(jnp.int32).astype(jnp.int16)


def code(mine, got):
    return pl.pallas_call(
        code_kernel,
        out_shape=jax.ShapeDtypeStruct((mine.shape[0] + TAIL, BATCH), jnp.int16),
        in_specs=vmem(2),
        out_specs=pl.BlockSpec(memory_space=pltpu.VMEM),
        cost_estimate=pl.CostEstimate(flops=1000, bytes_accessed=1 << 20, transcendentals=0),
        compiler_params=params(),
        name="code",
    )(mine, got)


def total(mine, got, far, at):
    rows = mine.shape[0]
    spot = rows + at.start // BLOCK * (TAIL // 8)
    scale = jnp.exp2(far[spot : spot + 1, :].astype(jnp.int32).astype(F32))
    other = far[at, :].astype(jnp.int32).astype(F32) * scale
    return (mine[at, :BATCH] + got[at, :BATCH] + other).T.astype(BF16)


def finish_kernel(*refs):
    out_ref, (mine, got, far) = refs[-1], refs[-4:-1]
    first = out_ref.shape[0] - BATCH
    if first:
        out_ref[:first, :] = refs[0][...]
    for r in range(mine.shape[0] // BLOCK):
        at = slice(r * BLOCK, (r + 1) * BLOCK)
        out_ref[first:, at] = total(mine, got, far, at)


def finish(parts, before=()):
    rows = parts[0].shape[0]
    return pl.pallas_call(
        finish_kernel,
        out_shape=jax.ShapeDtypeStruct(((1 + len(before)) * BATCH, rows), BF16),
        in_specs=vmem(3 + len(before)),
        out_specs=pl.BlockSpec(memory_space=pltpu.VMEM),
        cost_estimate=pl.CostEstimate(flops=1000000, bytes_accessed=3 << 20, transcendentals=0),
        compiler_params=params(),
    )(*before, *parts)


def on_device(integrals, block_mask, amplitudes, pair_batches):
    own = pick(amplitudes, pair_batches)
    near = send(own, ZX)
    xp0, yp0 = send(own, XM), send(own, YM)
    xm0, ym0 = send(own, XP), send(own, YP)
    near_a, near_b = halves([[(0, 0)], [(0, HALF)]], [near])
    xp1, yp1 = send(near_a, XM), send(near_b, YM)
    xm1, ym1 = send(near_a, XP), send(near_b, YP)
    plan = [[(0, 0)], [(1, HALF)], [(0, HALF)], [(1, 0)], [(0, HALF), (2, HALF)], [(1, 0), (3, 0)]]
    xa, yb, xb, ya, zx, zy = halves(plan, [xm0, ym0, xp0, yp0])
    x20, y20 = send(xa, XP), send(yb, YP)
    x21, y21 = send(xp1, XM), send(yp1, YM)
    x20b, y20a = send(xb, XP), send(ya, YP)
    zx, zy = send(zx, ZX), send(zy, ZX)
    zd = send(halves([[(0, 0), (1, 0)]], [x20b, y20a])[0], ZX)

    early_x = lay((0, 1, 2, 3), 0, [xm0, xm1, xp0, xp1])
    early_y = lay((0, 1, 2, 3), HALF, [ym0, ym1, yp0, yp1])
    along_x = lay((4, 5), 0, [x20, x21], early_x)
    along_y = lay((4, 5), HALF, [y20, y21], early_y)

    pieces = []
    for k in range(2):
        ym, yp = send(along_x[k], YP), send(along_x[k], YM)
        xm, xp = send(along_y[k], XP), send(along_y[k], XM)
        if k == 0:
            y2, x2 = send(ym, YP), send(xm, XP)
        else:
            y2, x2 = send(yp, YM), send(xp, XM)
        pieces.append(([ym, yp, y2], [xm, xp, x2]))

    v = [keep(4 * k, 4, integrals, block_mask) for k in range(2)]
    near_at = [(0, 0, 0), (0, 1, 0), (-1, 0, 0), (1, 0, 0), (0, 0, -1), (0, 0, 1)]
    arrays = [own, near, xm0, xp0, ym0, yp0]
    acc = cross(near_at, [[(i, None)] for i in range(6)], arrays, v)
    far_at = [(-1, 1, 0), (1, 1, 0), (0, 1, -1), (0, 1, 1), (2, 0, 0), (2, 1, 0), (0, 0, 2), (0, 1, 2)]
    arrays = [zx, zy, zd, xm1, xp1, ym1, yp1, x20, x20b, x21, y20a, y20, y21]
    picks = [
        [(3, None), (0, 0)],
        [(4, None), (0, 1)],
        [(1, 0), (5, None)],
        [(1, 1), (6, None)],
        [(7, None), (8, None)],
        [(9, None), (2, 0)],
        [(10, None), (11, None)],
        [(2, 1), (12, None)],
    ]
    acc = cross(far_at, picks, arrays, v, [acc])

    parts = []
    for k in range(2):
        ys, xs = pieces[k]
        if k == 0:
            theirs = group(0, False, LINE, ys, v, acc)
        else:
            begun = group(1, False, (1,), ys[1:2], v, acc)
            theirs = group(0, False, (-1, 2), ys[::2], v, begun)
        got = lax.ppermute(theirs, "grp", CORE)
        if k == 0:
            mine = group(2, True, LINE, xs, v, acc)
        else:
            begun = group(3, True, (1,), xs[1:2], v, acc)
            mine = group(0, True, (-1, 2), xs[::2], v, begun)
        packed = code(mine, got)
        far = lax.ppermute(packed, "grp", ZHI)
        parts += [mine, got, far]
    return finish(parts[3:], [finish(parts[:3])])


def solution(mesh):
    in_specs = (P("blk", "grp"), P("blk", "grp"), P(("grp", "blk"), None), P())
    out_specs = P("grp", "blk")

    return jax.shard_map(on_device, mesh=mesh, in_specs=in_specs, out_specs=out_specs, check_vma=False)
```
